32 devices in a mesh: dp: 8 (over y, x, core), space: 4 (over z).
Axes of the slice: x: 2, y: 2, z: 4, core: 2. Of those that a mesh axis runs over, the one named last changes fastest.
Arguments:
- volume: bfloat16 [8, 8, 8, 8, 512], P('dp', 'space'), may hold values from -6 to 6
- conv_one: bfloat16 [3, 3, 3, 512, 256], P(None, None, None, 'dp'), may hold values from -0.125 to 0.125
- mix_one: bfloat16 [256, 256], P('dp'), may hold values from -0.375 to 0.375
- conv_two: bfloat16 [3, 3, 3, 256, 128], P(None, None, None, 'dp'), may hold values from -0.1875 to 0.1875
- mix_two: bfloat16 [128, 128], P('dp'), may hold values from -0.5 to 0.5
Outputs:
- decoded: bfloat16 [8, 32, 32, 32, 128], P('dp', 'space')
The draws below stay inside these ranges and needn't reach their ends.
All inputs are finite; a program needn't handle non-finite values.
Results may differ from the reference program's by a relative error of at most 0.007.
Values may be sent and summed in bfloat16 or wider, within the bound.
A program may use at most 64 MiB of HBM per device.

```python
import jax
import jax.numpy as jnp
from jax import lax

C0 = 512
C1 = 256
C2 = 128
H_IN = 8
W_IN = 8
DEPTH = 8
SAMPLES = 8


def level_of(rng, extent, pieces, low, high):
    def one(dim, shards_of):
        heights = jax.random.uniform(jax.random.fold_in(jax.random.fold_in(rng, 6), dim), (shards_of,), jnp.float32, low / len(pieces), high / len(pieces))
        return jnp.repeat(jnp.exp(heights), extent[dim] // shards_of).reshape((-1,) + (1,) * (len(extent) - dim - 1))

    gain = one(*pieces[0])
    for cut in pieces[1:]:
        gain = gain * one(*cut)
    return gain


def normal_values(stream_key, dims, width, limit, cuts=(), dtype=jnp.bfloat16):
    entries = width * jax.random.normal(stream_key, dims, jnp.float32)
    if cuts:
        entries = entries * level_of(stream_key, dims, cuts, -0.22, 0.18)
    return jnp.clip(entries, -limit, limit).astype(dtype)


def setup_inputs(seed: int = 0) -> dict:
    key_list = jax.random.split(jax.random.key(seed), 6)
    volume = normal_values(key_list[0], (SAMPLES, DEPTH, H_IN, W_IN, C0), 1.0, 6.0, ((0, 8), (1, 4)))
    conv_one = normal_values(key_list[1], (3, 3, 3, C0, C1), (4 * C0) ** -0.5, 0.125, ((3, 8),))
    mix_one = normal_values(key_list[2], (C1, C1), C1 ** -0.5, 0.375, ((0, 8),))
    conv_two = normal_values(key_list[3], (3, 3, 3, C1, C2), (4 * C1) ** -0.5, 0.1875, ((3, 8),))
    mix_two = normal_values(key_list[4], (C2, C2), C2 ** -0.5, 0.5, ((0, 8),))
    return dict(volume=volume, conv_one=conv_one, mix_one=mix_one, conv_two=conv_two, mix_two=mix_two)


PHASE_TAPS = (((1, 0),), ((2, 0), (0, 1)))


def phase_sum(padded, weight, planes, height, breadth, depth_taps):
    chans_in = padded.shape[-1]
    chans_out = weight.shape[-1]
    groups = []
    for taps_depth in depth_taps:
        for taps_rows in PHASE_TAPS:
            for taps_cols in PHASE_TAPS:
                total = None
                for depth_tap, depth_shift in taps_depth:
                    for row_tap, row_shift in taps_rows:
                        for col_tap, col_shift in taps_cols:
                            piece = padded[depth_shift:depth_shift + planes, row_shift:row_shift + height, col_shift:col_shift + breadth]
                            term = jnp.dot(piece.reshape(-1, chans_in), weight[depth_tap, row_tap, col_tap], preferred_element_type=jnp.float32)
                            total = term if total is None else total + term
                groups.append(total)
    return jnp.stack(groups).reshape(len(depth_taps), 2, 2, planes, height, breadth, chans_out)


def alternate(phased):
    planes, height, breadth, chans = phased.shape[3:]
    return jnp.transpose(phased, (3, 0, 4, 1, 5, 2, 6)).reshape(2 * planes, 2 * height, 2 * breadth, chans)


def up_block(field, weight, mixing):
    planes, height, breadth, chans = field.shape
    padded = jnp.pad(field, ((0, 1), (0, 1), (0, 1), (0, 0)))
    conv = alternate(phase_sum(padded, weight, planes, height, breadth, PHASE_TAPS))
    act = jax.nn.silu(conv).astype(jnp.bfloat16)
    mixed = jnp.dot(act.reshape(-1, act.shape[-1]), mixing, preferred_element_type=jnp.float32)
    return mixed.astype(jnp.bfloat16).reshape(conv.shape[:-1] + (mixing.shape[1],))


def reference(volume, conv_one, mix_one, conv_two, mix_two):
    def one_sample(sample):
        return up_block(up_block(sample, conv_one, mix_one), conv_two, mix_two)
    return lax.map(one_sample, volume)
```

```python
import functools

import jax
import jax.numpy as jnp
from jax import lax
from jax.experimental import pallas as pl
from jax.experimental.pallas import tpu as pltpu
from jax.sharding import PartitionSpec as P

MESH = pl.DeviceIdType.MESH
BF = jnp.bfloat16
F32 = jnp.float32
PHASE_TAPS = (((1, 0),), ((2, 0), (0, 1)))
DEPTH_TAPS = (1, 2, 0)


def taps_of(pd, pr, pc):
    for kd, sd in PHASE_TAPS[pd]:
        for kr, sr in PHASE_TAPS[pr]:
            for kc, sc in PHASE_TAPS[pc]:
                yield kd * 9 + kr * 3 + kc, sd * 4 + sr * 2 + sc


def silu(v):
    return v / (1.0 + jnp.exp(-v))


def first_kernel(
    n_dp, n_space, vol, w1, m1, w2, m2,
    up, w2all, m2all,
    gat, m1all, m1s, volx, pad, xs, act_all, act_in, upf, halo,
    ssem, rsem, fssem, frsem, vs, vr, hs, hr, asem, arsem, us, ur,
):
    n = n_dp // 2
    me = lax.axis_index("dp")
    s = lax.axis_index("space")
    q, core = me // 2, lax.rem(me, 2)
    sib = q * 2 + (1 - core)
    h = lax.rem(s, 2)
    mate = s + 1 - 2 * h
    base = s - h

    def peer(k):
        return lax.rem(q + k, n) * 2 + core

    def source(k):
        return lax.rem(q + n - k, n) * 2 + core

    def sib_source(k):
        return lax.rem(q + n - k, n) * 2 + (1 - core)

    barrier = pltpu.get_barrier_semaphore()
    for k in range(1, n):
        pl.semaphore_signal(barrier, inc=1, device_id={"dp": peer(k)}, device_id_type=MESH)
    pl.semaphore_signal(barrier, inc=1, device_id={"dp": sib}, device_id_type=MESH)
    for k in range(1, n_space):
        pl.semaphore_signal(
            barrier, inc=1, device_id={"space": lax.rem(s + k, n_space)}, device_id_type=MESH
        )
    pl.semaphore_wait(barrier, n + n_space - 1)

    lanes = pl.ds(pl.multiple_of(h * 128, 128), 128)

    def ends(item, slot):
        if item < 3:
            rows = pl.ds(DEPTH_TAPS[item] * 9, 9)
            return w1.at[rows, :, lanes], gat.at[slot, rows]
        mine, every = ((m1, m1all), (w2, w2all), (m2, m2all))[item - 3]
        return mine, every.at[slot]

    def to_peer(item, k):
        src, dst = ends(item, me)
        return pltpu.make_async_remote_copy(
            src, dst, ssem.at[item, k], rsem.at[item, k],
            device_id={"dp": peer(k)}, device_id_type=MESH,
        )

    def to_sib(item, k):
        if k == 0:
            src, dst = ends(item, me)
        else:
            _, dst = ends(item, source(k))
            src = dst
        return pltpu.make_async_remote_copy(
            src, dst, fssem.at[item, k], frsem.at[item, k],
            device_id={"dp": sib}, device_id_type=MESH,
        )

    def send(item):
        for k in range(1, n):
            to_peer(item, k).start()
        to_sib(item, 0).start()

    def forward(item):
        for k in range(1, n):
            to_peer(item, k).wait_recv()
            to_sib(item, k).start()

    def settle(item):
        for k in range(n):
            to_sib(item, k).wait_recv()

    def to_mate():
        return pltpu.make_async_remote_copy(
            vol, volx.at[pl.ds(2 * h, 2)], vs.at[0], vr.at[0],
            device_id={"space": mate}, device_id_type=MESH,
        )

    def vol_halo(j):
        return pltpu.make_async_remote_copy(
            vol.at[pl.ds(0, 1)], volx.at[pl.ds(4, 1)], hs.at[j], hr.at[0],
            device_id={"space": s - 1 - j}, device_id_type=MESH,
        )

    gives = jnp.logical_and(h == 0, s >= 2)
    takes = base + 2 < n_space

    to_mate().start()

    @pl.when(gives)
    def _():
        vol_halo(0).start()
        vol_halo(1).start()

    for item in (0, 3, 1, 2):
        send(item)

    gat[me] = w1[:, :, lanes]
    m1all[me] = m1[...]
    w2all[me] = w2[...]
    m2all[me] = m2[...]
    volx[pl.ds(2 * h, 2)] = vol[...]

    to_mate().wait_recv()

    @pl.when(takes)
    def _():
        vol_halo(0).wait_recv()

    @pl.when(jnp.logical_not(takes))
    def _():
        volx[pl.ds(4, 1)] = jnp.zeros((1,) + volx.shape[1:], BF)

    pad[:, :, 8:9] = jnp.zeros((2, 5, 1) + pad.shape[3:], F32)
    x = volx[...].astype(F32)
    pad[0, :, 0:8] = x
    pad[1, :, 0:8] = jnp.concatenate([x[:, :, 1:], jnp.zeros_like(x[:, :, :1])], 2)
    for sd in range(2):
        for sr in range(2):
            for sc in range(2):
                v = pad[sc, sd : sd + 4, sr : sr + 8]
                xs[sd * 4 + sr * 2 + sc] = v.reshape(256, v.shape[-1]).astype(BF)

    def to_act(p):
        return pltpu.make_async_remote_copy(
            act_all.at[p, 1 - h], act_in.at[p], asem.at[p], arsem.at[p],
            device_id={"space": mate}, device_id_type=MESH,
        )

    def conv_phase(p):
        acc = None
        for t, sh in taps_of(p // 4, p // 2 % 2, p % 2):
            w = gat[:, t].reshape(-1, 128)
            term = jnp.dot(xs[sh], w, preferred_element_type=F32)
            acc = term if acc is None else acc + term
        act_all[p] = silu(acc).astype(BF).reshape(2, 128, 128)
        to_act(p).start()

    def mix_phase(p):
        pd, pr, pc = p // 4, p // 2 % 2, p % 2
        to_act(p).wait_recv()
        r = jnp.dot(act_all[p, h], m1s[h], preferred_element_type=F32)
        r = r + jnp.dot(act_in[p], m1s[1 - h], preferred_element_type=F32)
        for d in range(2):
            for i in range(8):
                row = d * 64 + i * 8
                for half in range(2):
                    upf[2 * d + pd, 2 * i + pr, half, pl.ds(pc, 8, stride=2), :] = r[
                        row : row + 8, half * 128 : half * 128 + 128
                    ]

    forward(0)
    forward(3)
    settle(0)
    for p in range(4):
        conv_phase(p)
    forward(1)
    forward(2)
    send(4)
    send(5)
    settle(3)
    m1s[...] = m1all[...].reshape(2, 128, 256)
    for p in range(4):
        mix_phase(p)

    def emit(plane):
        for half in range(2):
            up[plane, 0:16, :, half * 128 : half * 128 + 128] = upf[plane, :, half].astype(BF)

    emit(0)

    def up_halo():
        return pltpu.make_async_remote_copy(
            up.at[0, pl.ds(0, 16)], halo, us.at[0], ur.at[0],
            device_id={"space": s - 1}, device_id_type=MESH,
        )

    @pl.when(s > 0)
    def _():
        up_halo().start()

    settle(1)
    settle(2)
    for p in range(4, 8):
        conv_phase(p)
    forward(4)
    forward(5)
    for p in range(4, 8):
        mix_phase(p)
    for plane in range(1, 4):
        emit(plane)
    up[:, 16:17] = jnp.zeros((5, 1) + up.shape[2:], BF)

    last = s + 1 == n_space

    @pl.when(last)
    def _():
        up[4, 0:16] = jnp.zeros(halo.shape, BF)

    @pl.when(jnp.logical_not(last))
    def _():
        up_halo().wait_recv()
        up[4, 0:16] = halo[...]

    settle(4)
    settle(5)
    for item in range(6):
        for k in range(n):
            if k:
                to_peer(item, k).wait_send()
            to_sib(item, k).wait_send()
    to_mate().wait_send()
    for p in range(8):
        to_act(p).wait_send()

    @pl.when(gives)
    def _():
        vol_halo(0).wait_send()
        vol_halo(1).wait_send()

    @pl.when(s > 0)
    def _():
        up_halo().wait_send()


def second_kernel(up, w2, m2, out, wide, xs):
    d = pl.program_id(0)
    for sd in range(2):
        x = up[d + sd]
        moved = x.astype(F32)
        moved = jnp.concatenate([moved[:, 1:], jnp.zeros_like(moved[:, :1])], 1).astype(BF)
        for sr in range(2):
            xs[sd * 4 + sr * 2] = x[sr : sr + 16].reshape(256, 256)
            xs[sd * 4 + sr * 2 + 1] = moved[sr : sr + 16].reshape(256, 256)
    mixing = m2[...].reshape(128, 128)
    for p in range(8):
        pd, pr, pc = p // 4, p // 2 % 2, p % 2
        acc = None
        for t, sh in taps_of(pd, pr, pc):
            term = jnp.dot(xs[sh], w2[:, t].reshape(256, 128), preferred_element_type=F32)
            acc = term if acc is None else acc + term
        r = jnp.dot(silu(acc).astype(BF), mixing, preferred_element_type=F32)
        for i in range(16):
            wide[pd, 2 * i + pr, pl.ds(pc, 16, stride=2), :] = r[i * 16 : i * 16 + 16]
    out[...] = wide[...].astype(BF)


def per_device(n_dp, n_space, volume, conv_one, mix_one, conv_two, mix_two):
    n = n_dp // 2
    w1 = conv_one.reshape((27,) + conv_one.shape[3:])
    w2 = conv_two.reshape((27,) + conv_two.shape[3:])
    vm = pl.BlockSpec(memory_space=pltpu.VMEM)
    dma = pltpu.SemaphoreType.DMA
    up, w2all, m2all = pl.pallas_call(
        functools.partial(first_kernel, n_dp, n_space),
        out_shape=(
            jax.ShapeDtypeStruct((5, 17, 16, 256), BF),
            jax.ShapeDtypeStruct((n_dp,) + w2.shape, BF),
            jax.ShapeDtypeStruct((n_dp,) + mix_two.shape, BF),
        ),
        in_specs=[vm] * 5,
        out_specs=(vm,) * 3,
        scratch_shapes=[
            pltpu.VMEM((n_dp, 27, w1.shape[1], 128), BF),
            pltpu.VMEM((n_dp,) + mix_one.shape, BF),
            pltpu.VMEM((2, 128, 256), BF),
            pltpu.VMEM((5, 8, 8, 512), BF),
            pltpu.VMEM((2, 5, 9, 8, 512), F32),
            pltpu.VMEM((8, 256, 512), BF),
            pltpu.VMEM((8, 2, 128, 128), BF),
            pltpu.VMEM((8, 128, 128), BF),
            pltpu.VMEM((4, 16, 2, 16, 128), F32),
            pltpu.VMEM((16, 16, 256), BF),
            dma((6, n)), dma((6, n)), dma((6, n)), dma((6, n)),
            dma((1,)), dma((1,)), dma((2,)), dma((1,)),
            dma((8,)), dma((8,)), dma((1,)), dma((1,)),
        ],
        compiler_params=pltpu.CompilerParams(
            collective_id=0, has_side_effects=True, vmem_limit_bytes=48 * 2**20
        ),
    )(volume[0], w1, mix_one, w2, mix_two)
    whole = lambda shape: pl.BlockSpec(shape, lambda d: (0,) * len(shape))
    decoded = pl.pallas_call(
        second_kernel,
        grid=(4,),
        out_shape=jax.ShapeDtypeStruct((8, 32, 32, 128), BF),
        in_specs=[whole(up.shape), whole(w2all.shape), whole(m2all.shape)],
        out_specs=pl.BlockSpec((2, 32, 32, 128), lambda d: (d, 0, 0, 0)),
        scratch_shapes=[pltpu.VMEM((2, 32, 32, 128), F32), pltpu.VMEM((8, 256, 256), BF)],
        compiler_params=pltpu.CompilerParams(vmem_limit_bytes=40 * 2**20),
    )(up, w2all, m2all)
    return decoded[None]


def solution(mesh):
    return jax.shard_map(
        functools.partial(per_device, mesh.shape["dp"], mesh.shape["space"]),
        mesh=mesh,
        in_specs=(
            P("dp", "space", None, None, None),
            P(None, None, None, "dp", None),
            P("dp", None),
            P(None, None, None, "dp", None),
            P("dp", None),
        ),
        out_specs=P("dp", "space", None, None, None),
        check_vma=False,
    )
```

```python
import functools

import jax
import jax.numpy as jnp
from jax import lax
from jax.experimental import pallas as pl
from jax.experimental.pallas import tpu as pltpu
from jax.sharding import PartitionSpec as P

MESH = pl.DeviceIdType.MESH
BF = jnp.bfloat16
F32 = jnp.float32
PHASE_TAPS = (((1, 0),), ((2, 0), (0, 1)))
DEPTH_TAPS = (1, 2, 0)


def silu(v):
    u = 0.5 * v
    return u + u * jnp.tanh(u)


def pair_sum(xs, weight, pd, pr):
    both, extra = None, None
    for kd, sd in PHASE_TAPS[pd]:
        for kr, sr in PHASE_TAPS[pr]:
            t, sh = kd * 9 + kr * 3, sd * 4 + sr * 2
            wide = jnp.concatenate([weight(t + 1), weight(t + 2)], 1)
            a = jnp.dot(xs[sh], wide, preferred_element_type=F32)
            b = jnp.dot(xs[sh + 1], weight(t), preferred_element_type=F32)
            both = a if both is None else both + a
            extra = b if extra is None else extra + b
    return both[:, :128], both[:, 128:] + extra


def first_kernel(
    n_dp, n_space, vol, w1, m1, w2, m2,
    up, w2all, m2all,
    gat, m1all, m1s, volx, pad, xs, act_all, act_in, upf, halo,
    ssem, rsem, fssem, frsem, vs, vr, hs, hr, asem, arsem, us, ur, own,
):
    n = n_dp // 2
    me = lax.axis_index("dp")
    s = lax.axis_index("space")
    q, core = me // 2, lax.rem(me, 2)
    sib = q * 2 + (1 - core)
    h = lax.rem(s, 2)
    mate = s + 1 - 2 * h
    base = s - h

    def peer(k):
        return lax.rem(q + k, n) * 2 + core

    def source(k):
        return lax.rem(q + n - k, n) * 2 + core

    def sib_source(k):
        return lax.rem(q + n - k, n) * 2 + (1 - core)

    barrier = pltpu.get_barrier_semaphore()
    for k in range(1, n):
        pl.semaphore_signal(barrier, inc=1, device_id={"dp": peer(k)}, device_id_type=MESH)
    pl.semaphore_signal(barrier, inc=1, device_id={"dp": sib}, device_id_type=MESH)
    for k in range(1, n_space):
        pl.semaphore_signal(
            barrier, inc=1, device_id={"space": lax.rem(s + k, n_space)}, device_id_type=MESH
        )
    pl.semaphore_wait(barrier, n + n_space - 1)

    lanes = pl.ds(pl.multiple_of(h * 128, 128), 128)

    def ends(item, slot):
        if item < 3:
            rows = pl.ds(DEPTH_TAPS[item] * 9, 9)
            return w1.at[rows, :, lanes], gat.at[slot, rows]
        mine, every = ((m1, m1all), (w2, w2all), (m2, m2all))[item - 3]
        return mine, every.at[slot]

    def to_peer(item, k):
        src, dst = ends(item, me)
        return pltpu.make_async_remote_copy(
            src, dst, ssem.at[item, k], rsem.at[item, k],
            device_id={"dp": peer(k)}, device_id_type=MESH,
        )

    def to_sib(item, k):
        if k == 0:
            src, dst = ends(item, me)
        else:
            _, dst = ends(item, source(k))
            src = dst
        return pltpu.make_async_remote_copy(
            src, dst, fssem.at[item, k], frsem.at[item, k],
            device_id={"dp": sib}, device_id_type=MESH,
        )

    flip = {
        1: q + 1 - 2 * lax.rem(q, 2),
        2: q + 2 - 4 * lax.rem(q // 2, 2),
    }

    def crosses(item):
        return n == 4 and item in (0, 1, 2, 4)

    def straight(item, k):
        src, dst = ends(item, me)
        return pltpu.make_async_remote_copy(
            src, dst, ssem.at[item, k], rsem.at[item, k],
            device_id={"dp": flip[k] * 2 + core}, device_id_type=MESH,
        )

    def half_of(item, chip, j):
        slot = chip * 2 + core
        if item < 3:
            rows = gat.shape[2] // 2
            return gat.at[slot, pl.ds(DEPTH_TAPS[item] * 9, 9), pl.ds(j * rows, rows)]
        return w2all.at[slot, pl.ds(14 * j, 14 - j)]

    def around(item, k):
        ref = half_of(item, flip[k], k - 1)
        sem = 3 * (k - 1)
        return pltpu.make_async_remote_copy(
            ref, ref, ssem.at[item, sem], rsem.at[item, sem],
            device_id={"dp": flip[3 - k] * 2 + core}, device_id_type=MESH,
        )

    def sib_from(item, k):
        chip = q if k == 0 else 3 - q if k == 3 else flip[k]
        src, dst = ends(item, chip * 2 + core)
        return pltpu.make_async_remote_copy(
            src if k == 0 else dst, dst, fssem.at[item, k], frsem.at[item, k],
            device_id={"dp": sib}, device_id_type=MESH,
        )

    def core_copy(item, k):
        return sib_from(item, k) if crosses(item) else to_sib(item, k)

    def send(item):
        if crosses(item):
            for k in (1, 2):
                straight(item, k).start()
        else:
            for k in range(1, n):
                to_peer(item, k).start()
        core_copy(item, 0).start()

    def forward(item):
        if crosses(item):
            for k in (1, 2):
                straight(item, k).wait_recv()
                around(item, k).start()
                core_copy(item, k).start()
        else:
            for k in range(1, n):
                to_peer(item, k).wait_recv()
                core_copy(item, k).start()

    def across(item):
        if crosses(item):
            for k in (1, 2):
                around(item, k).wait_recv()
            core_copy(item, 3).start()

    def settle(item):
        for k in range(n):
            core_copy(item, k).wait_recv()

    def to_mate():
        return pltpu.make_async_remote_copy(
            vol, volx.at[pl.ds(2 * h, 2)], vs.at[0], vr.at[0],
            device_id={"space": mate}, device_id_type=MESH,
        )

    def vol_halo(j):
        return pltpu.make_async_remote_copy(
            vol.at[pl.ds(0, 1)], volx.at[pl.ds(4, 1)], hs.at[j], hr.at[0],
            device_id={"space": s - 1 - j}, device_id_type=MESH,
        )

    gives = jnp.logical_and(h == 0, s >= 2)
    takes = base + 2 < n_space

    to_mate().start()

    @pl.when(gives)
    def _():
        vol_halo(0).start()
        vol_halo(1).start()

    for item in (0, 3, 1):
        send(item)

    owned = [
        pltpu.make_async_copy(src, dst, own.at[i])
        for i, (src, dst) in enumerate((
            (vol, volx.at[pl.ds(2 * h, 2)]),
            (w1.at[:, :, lanes], gat.at[me]),
            (m1, m1all.at[me]),
            (w2, w2all.at[me]),
            (m2, m2all.at[me]),
        ))
    ]
    for copy in owned:
        copy.start()
    owned[0].wait()
    to_mate().wait_recv()

    @pl.when(takes)
    def _():
        vol_halo(0).wait_recv()

    @pl.when(jnp.logical_not(takes))
    def _():
        volx[pl.ds(4, 1)] = jnp.zeros((1,) + volx.shape[1:], BF)

    pad[:, :, 8:9] = jnp.zeros((2, 5, 1) + pad.shape[3:], F32)
    x = volx[...].astype(F32)
    pad[0, :, 0:8] = x
    pad[1, :, 0:8] = jnp.concatenate([x[:, :, 1:], jnp.zeros_like(x[:, :, :1])], 2)
    for sd in range(2):
        for sr in range(2):
            for sc in range(2):
                v = pad[sc, sd : sd + 4, sr : sr + 8]
                xs[sd * 4 + sr * 2 + sc] = v.reshape(256, v.shape[-1]).astype(BF)

    def to_act(p):
        return pltpu.make_async_remote_copy(
            act_all.at[p, 1 - h], act_in.at[p], asem.at[p], arsem.at[p],
            device_id={"space": mate}, device_id_type=MESH,
        )

    def conv_pair(pd, pr):
        weight = lambda t: gat[:, t].reshape(-1, 128)
        for pc, acc in enumerate(pair_sum(xs, weight, pd, pr)):
            p = pd * 4 + pr * 2 + pc
            act_all[p] = silu(acc).astype(BF).reshape(2, 128, 128)
            to_act(p).start()

    def mix_phase(p):
        pd, pr, pc = p // 4, p // 2 % 2, p % 2
        to_act(p).wait_recv()
        r = jnp.dot(act_all[p, h], m1s[h], preferred_element_type=F32)
        r = r + jnp.dot(act_in[p], m1s[1 - h], preferred_element_type=F32)
        for d in range(2):
            for i in range(8):
                row = d * 64 + i * 8
                for half in range(2):
                    upf[2 * d + pd, 2 * i + pr, half, pl.ds(pc, 8, stride=2), :] = r[
                        row : row + 8, half * 128 : half * 128 + 128
                    ]

    forward(0)
    send(2)
    across(0)
    for copy in owned[1:]:
        copy.wait()
    forward(1)
    settle(0)
    conv_pair(0, 0)
    conv_pair(0, 1)
    forward(2)
    send(4)
    send(5)
    forward(3)
    across(1)
    across(2)
    settle(3)
    m1s[...] = m1all[...].reshape(2, 128, 256)
    for p in range(4):
        mix_phase(p)

    def emit(plane):
        for half in range(2):
            up[plane, 0:16, :, half * 128 : half * 128 + 128] = upf[plane, :, half].astype(BF)

    emit(0)

    def up_halo():
        return pltpu.make_async_remote_copy(
            up.at[0, pl.ds(0, 16)], halo, us.at[0], ur.at[0],
            device_id={"space": s - 1}, device_id_type=MESH,
        )

    @pl.when(s > 0)
    def _():
        up_halo().start()

    settle(1)
    settle(2)
    conv_pair(1, 0)
    conv_pair(1, 1)
    forward(4)
    forward(5)
    for p in range(4, 8):
        mix_phase(p)
    for plane in range(1, 4):
        emit(plane)
    up[:, 16:17] = jnp.zeros((5, 1) + up.shape[2:], BF)

    last = s + 1 == n_space

    @pl.when(last)
    def _():
        up[4, 0:16] = jnp.zeros(halo.shape, BF)

    @pl.when(jnp.logical_not(last))
    def _():
        up_halo().wait_recv()
        up[4, 0:16] = halo[...]

    across(4)
    settle(4)
    settle(5)
    for item in range(6):
        for k in range(n):
            core_copy(item, k).wait_send()
        if crosses(item):
            for k in (1, 2):
                straight(item, k).wait_send()
                around(item, k).wait_send()
        else:
            for k in range(1, n):
                to_peer(item, k).wait_send()
    to_mate().wait_send()
    for p in range(8):
        to_act(p).wait_send()

    @pl.when(gives)
    def _():
        vol_halo(0).wait_send()
        vol_halo(1).wait_send()

    @pl.when(s > 0)
    def _():
        up_halo().wait_send()


def second_kernel(up, w2, m2, out, wide, xs):
    d = pl.program_id(0)
    for sd in range(2):
        x = up[d + sd]
        moved = x.astype(F32)
        moved = jnp.concatenate([moved[:, 1:], jnp.zeros_like(moved[:, :1])], 1).astype(BF)
        for sr in range(2):
            xs[sd * 4 + sr * 2] = x[sr : sr + 16].reshape(256, 256)
            xs[sd * 4 + sr * 2 + 1] = moved[sr : sr + 16].reshape(256, 256)
    m = m2[...].reshape(128, 128)
    none = jnp.zeros_like(m)
    mixing = jnp.concatenate(
        [jnp.concatenate([m, none], 1), jnp.concatenate([none, m], 1)], 0
    )
    for pd in range(2):
        for pr in range(2):
            acc = jnp.concatenate(
                pair_sum(xs, lambda t: w2[:, t].reshape(256, 128), pd, pr), 1
            )
            r = jnp.dot(silu(acc).astype(BF), mixing, preferred_element_type=F32)
            for pc in range(2):
                for i in range(16):
                    wide[pd, 2 * i + pr, pl.ds(pc, 16, stride=2), :] = r[
                        i * 16 : i * 16 + 16, pc * 128 : pc * 128 + 128
                    ]
    out[...] = wide[...].astype(BF)


def per_device(n_dp, n_space, volume, conv_one, mix_one, conv_two, mix_two):
    n = n_dp // 2
    w1 = conv_one.reshape((27,) + conv_one.shape[3:])
    w2 = conv_two.reshape((27,) + conv_two.shape[3:])
    vm = pl.BlockSpec(memory_space=pltpu.VMEM)
    dma = pltpu.SemaphoreType.DMA
    up, w2all, m2all = pl.pallas_call(
        functools.partial(first_kernel, n_dp, n_space),
        out_shape=(
            jax.ShapeDtypeStruct((5, 17, 16, 256), BF),
            jax.ShapeDtypeStruct((n_dp,) + w2.shape, BF),
            jax.ShapeDtypeStruct((n_dp,) + mix_two.shape, BF),
        ),
        in_specs=[pl.BlockSpec(memory_space=pltpu.HBM)] * 5,
        out_specs=(vm,) * 3,
        scratch_shapes=[
            pltpu.VMEM((n_dp, 27, w1.shape[1], 128), BF),
            pltpu.VMEM((n_dp,) + mix_one.shape, BF),
            pltpu.VMEM((2, 128, 256), BF),
            pltpu.VMEM((5, 8, 8, 512), BF),
            pltpu.VMEM((2, 5, 9, 8, 512), F32),
            pltpu.VMEM((8, 256, 512), BF),
            pltpu.VMEM((8, 2, 128, 128), BF),
            pltpu.VMEM((8, 128, 128), BF),
            pltpu.VMEM((4, 16, 2, 16, 128), F32),
            pltpu.VMEM((16, 16, 256), BF),
            dma((6, n)), dma((6, n)), dma((6, n)), dma((6, n)),
            dma((1,)), dma((1,)), dma((2,)), dma((1,)),
            dma((8,)), dma((8,)), dma((1,)), dma((1,)), dma((5,)),
        ],
        compiler_params=pltpu.CompilerParams(
            collective_id=0, has_side_effects=True, vmem_limit_bytes=48 * 2**20
        ),
    )(volume[0], w1, mix_one, w2, mix_two)
    whole = lambda shape: pl.BlockSpec(shape, lambda d: (0,) * len(shape))
    decoded = pl.pallas_call(
        second_kernel,
        grid=(4,),
        out_shape=jax.ShapeDtypeStruct((8, 32, 32, 128), BF),
        in_specs=[whole(up.shape), whole(w2all.shape), whole(m2all.shape)],
        out_specs=pl.BlockSpec((2, 32, 32, 128), lambda d: (d, 0, 0, 0)),
        scratch_shapes=[pltpu.VMEM((2, 32, 32, 128), F32), pltpu.VMEM((8, 256, 256), BF)],
        compiler_params=pltpu.CompilerParams(vmem_limit_bytes=40 * 2**20),
    )(up, w2all, m2all)
    return decoded[None]


def solution(mesh):
    return jax.shard_map(
        functools.partial(per_device, mesh.shape["dp"], mesh.shape["space"]),
        mesh=mesh,
        in_specs=(
            P("dp", "space", None, None, None),
            P(None, None, None, "dp", None),
            P("dp", None),
            P(None, None, None, "dp", None),
            P("dp", None),
        ),
        out_specs=P("dp", "space", None, None, None),
        check_vma=False,
    )
```

```python
import functools

import jax
import jax.numpy as jnp
from jax import lax
from jax.experimental import pallas as pl
from jax.experimental.pallas import tpu as pltpu
from jax.sharding import PartitionSpec as P

MESH = pl.DeviceIdType.MESH
BF = jnp.bfloat16
F32 = jnp.float32
PHASE_TAPS = (((1, 0),), ((2, 0), (0, 1)))
DEPTH_TAPS = (1, 2, 0)


def silu(v):
    u = 0.5 * v
    return u + u * jnp.tanh(u)


def pair_sum(xs, weight, pd, pr):
    both, extra = None, None
    for kd, sd in PHASE_TAPS[pd]:
        for kr, sr in PHASE_TAPS[pr]:
            t, sh = kd * 9 + kr * 3, sd * 4 + sr * 2
            wide = jnp.concatenate([weight(t + 1), weight(t + 2)], 1)
            a = jnp.dot(xs[sh], wide, preferred_element_type=F32)
            b = jnp.dot(xs[sh + 1], weight(t), preferred_element_type=F32)
            both = a if both is None else both + a
            extra = b if extra is None else extra + b
    return both[:, :128], both[:, 128:] + extra


def fused_kernel(
    n_dp, n_space, vol, w1, m1, w2, m2,
    decoded,
    up, w2all, m2all, wide, views, planes, gat, m1all, m1s, volx, pad, xs, act_all, act_in, upf, halo,
    ssem, rsem, fssem, frsem, vs, vr, hs, hr, asem, arsem, us, ur, own, outsem,
):
    n = n_dp // 2
    me = lax.axis_index("dp")
    s = lax.axis_index("space")
    q, core = me // 2, lax.rem(me, 2)
    sib = q * 2 + (1 - core)
    h = lax.rem(s, 2)
    mate = s + 1 - 2 * h
    base = s - h

    def peer(k):
        return lax.rem(q + k, n) * 2 + core

    def source(k):
        return lax.rem(q + n - k, n) * 2 + core

    def sib_source(k):
        return lax.rem(q + n - k, n) * 2 + (1 - core)

    barrier = pltpu.get_barrier_semaphore()
    for k in range(1, n):
        pl.semaphore_signal(barrier, inc=1, device_id={"dp": peer(k)}, device_id_type=MESH)
    pl.semaphore_signal(barrier, inc=1, device_id={"dp": sib}, device_id_type=MESH)
    for k in range(1, n_space):
        pl.semaphore_signal(
            barrier, inc=1, device_id={"space": lax.rem(s + k, n_space)}, device_id_type=MESH
        )
    pl.semaphore_wait(barrier, n + n_space - 1)

    lanes = pl.ds(pl.multiple_of(h * 128, 128), 128)

    def ends(item, slot):
        if item < 3:
            rows = pl.ds(DEPTH_TAPS[item] * 9, 9)
            return w1.at[rows, :, lanes], gat.at[slot, rows]
        mine, every = ((m1, m1all), (w2, w2all), (m2, m2all))[item - 3]
        return mine, every.at[slot]

    def to_peer(item, k):
        src, dst = ends(item, me)
        return pltpu.make_async_remote_copy(
            src, dst, ssem.at[item, k], rsem.at[item, k],
            device_id={"dp": peer(k)}, device_id_type=MESH,
        )

    def to_sib(item, k):
        if k == 0:
            src, dst = ends(item, me)
        else:
            _, dst = ends(item, source(k))
            src = dst
        return pltpu.make_async_remote_copy(
            src, dst, fssem.at[item, k], frsem.at[item, k],
            device_id={"dp": sib}, device_id_type=MESH,
        )

    flip = {
        1: q + 1 - 2 * lax.rem(q, 2),
        2: q + 2 - 4 * lax.rem(q // 2, 2),
    }

    def crosses(item):
        return n == 4 and item in (0, 1, 2, 4)

    def straight(item, k):
        src, dst = ends(item, me)
        return pltpu.make_async_remote_copy(
            src, dst, ssem.at[item, k], rsem.at[item, k],
            device_id={"dp": flip[k] * 2 + core}, device_id_type=MESH,
        )

    def half_of(item, chip, j):
        slot = chip * 2 + core
        if item < 3:
            rows = gat.shape[2] // 2
            return gat.at[slot, pl.ds(DEPTH_TAPS[item] * 9, 9), pl.ds(j * rows, rows)]
        return w2all.at[slot, pl.ds(14 * j, 14 - j)]

    def around(item, k):
        ref = half_of(item, flip[k], k - 1)
        sem = 3 * (k - 1)
        return pltpu.make_async_remote_copy(
            ref, ref, ssem.at[item, sem], rsem.at[item, sem],
            device_id={"dp": flip[3 - k] * 2 + core}, device_id_type=MESH,
        )

    def sib_from(item, k):
        chip = q if k == 0 else 3 - q if k == 3 else flip[k]
        src, dst = ends(item, chip * 2 + core)
        return pltpu.make_async_remote_copy(
            src if k == 0 else dst, dst, fssem.at[item, k], frsem.at[item, k],
            device_id={"dp": sib}, device_id_type=MESH,
        )

    def core_copy(item, k):
        return sib_from(item, k) if crosses(item) else to_sib(item, k)

    def send(item):
        if crosses(item):
            for k in (1, 2):
                straight(item, k).start()
        else:
            for k in range(1, n):
                to_peer(item, k).start()
        core_copy(item, 0).start()

    def forward(item):
        if crosses(item):
            for k in (1, 2):
                straight(item, k).wait_recv()
                around(item, k).start()
                core_copy(item, k).start()
        else:
            for k in range(1, n):
                to_peer(item, k).wait_recv()
                core_copy(item, k).start()

    def across(item):
        if crosses(item):
            for k in (1, 2):
                around(item, k).wait_recv()
            core_copy(item, 3).start()

    def settle(item):
        for k in range(n):
            core_copy(item, k).wait_recv()

    def to_mate():
        return pltpu.make_async_remote_copy(
            vol, volx.at[pl.ds(2 * h, 2)], vs.at[0], vr.at[0],
            device_id={"space": mate}, device_id_type=MESH,
        )

    def vol_halo(j):
        return pltpu.make_async_remote_copy(
            vol.at[pl.ds(0, 1)], volx.at[pl.ds(4, 1)], hs.at[j], hr.at[0],
            device_id={"space": s - 1 - j}, device_id_type=MESH,
        )

    gives = jnp.logical_and(h == 0, s >= 2)
    takes = base + 2 < n_space

    to_mate().start()

    @pl.when(gives)
    def _():
        vol_halo(0).start()
        vol_halo(1).start()

    for item in (0, 3, 1):
        send(item)

    owned = [
        pltpu.make_async_copy(src, dst, own.at[i])
        for i, (src, dst) in enumerate((
            (vol, volx.at[pl.ds(2 * h, 2)]),
            (w1.at[:, :, lanes], gat.at[me]),
            (m1, m1all.at[me]),
            (w2, w2all.at[me]),
            (m2, m2all.at[me]),
        ))
    ]
    for copy in owned:
        copy.start()
    owned[0].wait()
    to_mate().wait_recv()

    @pl.when(takes)
    def _():
        vol_halo(0).wait_recv()

    @pl.when(jnp.logical_not(takes))
    def _():
        volx[pl.ds(4, 1)] = jnp.zeros((1,) + volx.shape[1:], BF)

    pad[:, :, 8:9] = jnp.zeros((2, 5, 1) + pad.shape[3:], F32)
    x = volx[...].astype(F32)
    pad[0, :, 0:8] = x
    pad[1, :, 0:8] = jnp.concatenate([x[:, :, 1:], jnp.zeros_like(x[:, :, :1])], 2)
    for sd in range(2):
        for sr in range(2):
            for sc in range(2):
                v = pad[sc, sd : sd + 4, sr : sr + 8]
                xs[sd * 4 + sr * 2 + sc] = v.reshape(256, v.shape[-1]).astype(BF)

    def to_act(p):
        return pltpu.make_async_remote_copy(
            act_all.at[p, 1 - h], act_in.at[p], asem.at[p], arsem.at[p],
            device_id={"space": mate}, device_id_type=MESH,
        )

    def conv_pair(pd, pr):
        weight = lambda t: gat[:, t].reshape(-1, 128)
        for pc, acc in enumerate(pair_sum(xs, weight, pd, pr)):
            p = pd * 4 + pr * 2 + pc
            act_all[p] = silu(acc).astype(BF).reshape(2, 128, 128)
            to_act(p).start()

    def mix_phase(p):
        pd, pr, pc = p // 4, p // 2 % 2, p % 2
        to_act(p).wait_recv()
        r = jnp.dot(act_all[p, h], m1s[h], preferred_element_type=F32)
        r = r + jnp.dot(act_in[p], m1s[1 - h], preferred_element_type=F32)
        for d in range(2):
            for i in range(8):
                row = d * 64 + i * 8
                for half in range(2):
                    upf[2 * d + pd, 2 * i + pr, half, pl.ds(pc, 8, stride=2), :] = r[
                        row : row + 8, half * 128 : half * 128 + 128
                    ]

    forward(0)
    send(2)
    across(0)
    for copy in owned[1:]:
        copy.wait()
    forward(1)
    settle(0)
    conv_pair(0, 0)
    conv_pair(0, 1)
    forward(2)
    send(4)
    send(5)
    forward(3)
    across(1)
    across(2)
    settle(3)
    m1s[...] = m1all[...].reshape(2, 128, 256)
    for p in range(4):
        mix_phase(p)

    def emit(plane):
        for half in range(2):
            up[plane, 0:16, :, half * 128 : half * 128 + 128] = upf[plane, :, half].astype(BF)

    emit(0)

    def up_halo():
        return pltpu.make_async_remote_copy(
            up.at[0, pl.ds(0, 16)], halo, us.at[0], ur.at[0],
            device_id={"space": s - 1}, device_id_type=MESH,
        )

    @pl.when(s > 0)
    def _():
        up_halo().start()

    settle(1)
    settle(2)
    conv_pair(1, 0)
    conv_pair(1, 1)
    forward(4)
    forward(5)
    for p in range(4, 8):
        mix_phase(p)
    for plane in range(1, 4):
        emit(plane)
    up[:, 16:17] = jnp.zeros((5, 1) + up.shape[2:], BF)

    last = s + 1 == n_space

    @pl.when(last)
    def _():
        up[4, 0:16] = jnp.zeros(halo.shape, BF)

    @pl.when(jnp.logical_not(last))
    def _():
        up_halo().wait_recv()
        up[4, 0:16] = halo[...]

    across(4)
    settle(4)
    settle(5)

    def to_decoded(d):
        return pltpu.make_async_copy(
            planes.at[d], decoded.at[pl.ds(2 * d, 2)], outsem.at[d]
        )

    @pl.loop(0, 4)
    def _(d):
        second_block(d, up, w2all, m2all, planes.at[d], wide, views)
        to_decoded(d).start()

    for item in range(6):
        for k in range(n):
            core_copy(item, k).wait_send()
        if crosses(item):
            for k in (1, 2):
                straight(item, k).wait_send()
                around(item, k).wait_send()
        else:
            for k in range(1, n):
                to_peer(item, k).wait_send()
    to_mate().wait_send()
    for p in range(8):
        to_act(p).wait_send()

    @pl.when(gives)
    def _():
        vol_halo(0).wait_send()
        vol_halo(1).wait_send()

    @pl.when(s > 0)
    def _():
        up_halo().wait_send()

    for d in range(4):
        to_decoded(d).wait()


def second_block(d, up, w2, m2, out, wide, xs):
    for sd in range(2):
        x = up[d + sd]
        moved = x.astype(F32)
        moved = jnp.concatenate([moved[:, 1:], jnp.zeros_like(moved[:, :1])], 1).astype(BF)
        for sr in range(2):
            xs[sd * 4 + sr * 2] = x[sr : sr + 16].reshape(256, 256)
            xs[sd * 4 + sr * 2 + 1] = moved[sr : sr + 16].reshape(256, 256)
    m = m2[...].reshape(128, 128)
    none = jnp.zeros_like(m)
    mixing = jnp.concatenate(
        [jnp.concatenate([m, none], 1), jnp.concatenate([none, m], 1)], 0
    )
    for pd in range(2):
        for pr in range(2):
            acc = jnp.concatenate(
                pair_sum(xs, lambda t: w2[:, t].reshape(256, 128), pd, pr), 1
            )
            r = jnp.dot(silu(acc).astype(BF), mixing, preferred_element_type=F32)
            for pc in range(2):
                for i in range(16):
                    wide[pd, 2 * i + pr, pl.ds(pc, 16, stride=2), :] = r[
                        i * 16 : i * 16 + 16, pc * 128 : pc * 128 + 128
                    ]
    out[...] = wide[...].astype(BF)


def per_device(n_dp, n_space, volume, conv_one, mix_one, conv_two, mix_two):
    n = n_dp // 2
    w1 = conv_one.reshape((27,) + conv_one.shape[3:])
    w2 = conv_two.reshape((27,) + conv_two.shape[3:])
    hbm = pl.BlockSpec(memory_space=pltpu.HBM)
    dma = pltpu.SemaphoreType.DMA
    decoded = pl.pallas_call(
        functools.partial(fused_kernel, n_dp, n_space),
        out_shape=jax.ShapeDtypeStruct((8, 32, 32, 128), BF),
        in_specs=[hbm] * 5,
        out_specs=hbm,
        scratch_shapes=[
            pltpu.VMEM((5, 17, 16, 256), BF),
            pltpu.VMEM((n_dp,) + w2.shape, BF),
            pltpu.VMEM((n_dp,) + mix_two.shape, BF),
            pltpu.VMEM((2, 32, 32, 128), F32),
            pltpu.VMEM((8, 256, 256), BF),
            pltpu.VMEM((4, 2, 32, 32, 128), BF),
            pltpu.VMEM((n_dp, 27, w1.shape[1], 128), BF),
            pltpu.VMEM((n_dp,) + mix_one.shape, BF),
            pltpu.VMEM((2, 128, 256), BF),
            pltpu.VMEM((5, 8, 8, 512), BF),
            pltpu.VMEM((2, 5, 9, 8, 512), F32),
            pltpu.VMEM((8, 256, 512), BF),
            pltpu.VMEM((8, 2, 128, 128), BF),
            pltpu.VMEM((8, 128, 128), BF),
            pltpu.VMEM((4, 16, 2, 16, 128), F32),
            pltpu.VMEM((16, 16, 256), BF),
            dma((6, n)), dma((6, n)), dma((6, n)), dma((6, n)),
            dma((1,)), dma((1,)), dma((2,)), dma((1,)),
            dma((8,)), dma((8,)), dma((1,)), dma((1,)), dma((5,)), dma((4,)),
        ],
        compiler_params=pltpu.CompilerParams(
            collective_id=0, has_side_effects=True, vmem_limit_bytes=60 * 2**20
        ),
    )(volume[0], w1, mix_one, w2, mix_two)
    return decoded[None]


def solution(mesh):
    return jax.shard_map(
        functools.partial(per_device, mesh.shape["dp"], mesh.shape["space"]),
        mesh=mesh,
        in_specs=(
            P("dp", "space", None, None, None),
            P(None, None, None, "dp", None),
            P("dp", None),
            P(None, None, None, "dp", None),
            P("dp", None),
        ),
        out_specs=P("dp", "space", None, None, None),
        check_vma=False,
    )
```

```python
import functools

import jax
import jax.numpy as jnp
from jax import lax
from jax.experimental import pallas as pl
from jax.experimental.pallas import tpu as pltpu
from jax.sharding import PartitionSpec as P

MESH = pl.DeviceIdType.MESH
BF = jnp.bfloat16
F32 = jnp.float32
PHASE_TAPS = (((1, 0),), ((2, 0), (0, 1)))
DEPTH_TAPS = (1, 2, 0)


def silu(v):
    u = 0.5 * v
    return u + u * jnp.tanh(u)


def pair_sum(xs, weight, pd, pr):
    both, extra = None, None
    for kd, sd in PHASE_TAPS[pd]:
        for kr, sr in PHASE_TAPS[pr]:
            t, sh = kd * 9 + kr * 3, sd * 4 + sr * 2
            wide = jnp.concatenate([weight(t + 1), weight(t + 2)], 1)
            a = jnp.dot(xs[sh], wide, preferred_element_type=F32)
            b = jnp.dot(xs[sh + 1], weight(t), preferred_element_type=F32)
            both = a if both is None else both + a
            extra = b if extra is None else extra + b
    return both[:, :128], both[:, 128:] + extra


def fused_kernel(
    n_dp, n_space, vol, w1, m1, w2, m2,
    decoded,
    up, w2all, m2all, wide, views, planes, gat, m1all, m1s, volx, pad, xs, act_all, act_in, upf, halo,
    ssem, rsem, fssem, frsem, vs, vr, hs, hr, asem, arsem, us, ur, own, outsem,
):
    n = n_dp // 2
    me = lax.axis_index("dp")
    s = lax.axis_index("space")
    q, core = me // 2, lax.rem(me, 2)
    sib = q * 2 + (1 - core)
    h = lax.rem(s, 2)
    mate = s + 1 - 2 * h
    base = s - h

    def peer(k):
        return lax.rem(q + k, n) * 2 + core

    def source(k):
        return lax.rem(q + n - k, n) * 2 + core

    def sib_source(k):
        return lax.rem(q + n - k, n) * 2 + (1 - core)

    barrier = pltpu.get_barrier_semaphore()
    for k in range(1, n):
        pl.semaphore_signal(barrier, inc=1, device_id={"dp": peer(k)}, device_id_type=MESH)
    pl.semaphore_signal(barrier, inc=1, device_id={"dp": sib}, device_id_type=MESH)
    for k in range(1, n_space):
        pl.semaphore_signal(
            barrier, inc=1, device_id={"space": lax.rem(s + k, n_space)}, device_id_type=MESH
        )
    pl.semaphore_wait(barrier, n + n_space - 1)

    lanes = pl.ds(pl.multiple_of(h * 128, 128), 128)

    def ends(item, slot):
        if item < 3:
            rows = pl.ds(DEPTH_TAPS[item] * 9, 9)
            return w1.at[rows, :, lanes], gat.at[slot, rows]
        mine, every = ((m1, m1all), (w2, w2all), (m2, m2all))[item - 3]
        return mine, every.at[slot]

    def to_peer(item, k):
        src, dst = ends(item, me)
        return pltpu.make_async_remote_copy(
            src, dst, ssem.at[item, k], rsem.at[item, k],
            device_id={"dp": peer(k)}, device_id_type=MESH,
        )

    def to_sib(item, k):
        if k == 0:
            src, dst = ends(item, me)
        else:
            _, dst = ends(item, source(k))
            src = dst
        return pltpu.make_async_remote_copy(
            src, dst, fssem.at[item, k], frsem.at[item, k],
            device_id={"dp": sib}, device_id_type=MESH,
        )

    flip = {
        1: q + 1 - 2 * lax.rem(q, 2),
        2: q + 2 - 4 * lax.rem(q // 2, 2),
    }

    def crosses(item):
        return n == 4 and item in (0, 1, 2, 4)

    def straight(item, k):
        src, dst = ends(item, me)
        return pltpu.make_async_remote_copy(
            src, dst, ssem.at[item, k], rsem.at[item, k],
            device_id={"dp": flip[k] * 2 + core}, device_id_type=MESH,
        )

    def half_of(item, chip, j):
        slot = chip * 2 + core
        if item < 3:
            rows = gat.shape[2] // 2
            return gat.at[slot, pl.ds(DEPTH_TAPS[item] * 9, 9), pl.ds(j * rows, rows)]
        return w2all.at[slot, pl.ds(14 * j, 14 - j)]

    def around(item, k):
        ref = half_of(item, flip[k], k - 1)
        sem = 3 * (k - 1)
        return pltpu.make_async_remote_copy(
            ref, ref, ssem.at[item, sem], rsem.at[item, sem],
            device_id={"dp": flip[3 - k] * 2 + core}, device_id_type=MESH,
        )

    def sib_from(item, k):
        chip = q if k == 0 else 3 - q if k == 3 else flip[k]
        src, dst = ends(item, chip * 2 + core)
        return pltpu.make_async_remote_copy(
            src if k == 0 else dst, dst, fssem.at[item, k], frsem.at[item, k],
            device_id={"dp": sib}, device_id_type=MESH,
        )

    def core_copy(item, k):
        return sib_from(item, k) if crosses(item) else to_sib(item, k)

    def send(item):
        if crosses(item):
            for k in (1, 2):
                straight(item, k).start()
        else:
            for k in range(1, n):
                to_peer(item, k).start()
        core_copy(item, 0).start()

    def forward(item):
        if crosses(item):
            for k in (1, 2):
                straight(item, k).wait_recv()
                around(item, k).start()
                core_copy(item, k).start()
        else:
            for k in range(1, n):
                to_peer(item, k).wait_recv()
                core_copy(item, k).start()

    def across(item):
        if crosses(item):
            for k in (1, 2):
                around(item, k).wait_recv()
            core_copy(item, 3).start()

    def settle(item):
        for k in range(n):
            core_copy(item, k).wait_recv()

    def to_mate():
        return pltpu.make_async_remote_copy(
            vol, volx.at[pl.ds(2 * h, 2)], vs.at[0], vr.at[0],
            device_id={"space": mate}, device_id_type=MESH,
        )

    def vol_halo(j):
        return pltpu.make_async_remote_copy(
            vol.at[pl.ds(0, 1)], volx.at[pl.ds(4, 1)], hs.at[j], hr.at[0],
            device_id={"space": s - 1 - j}, device_id_type=MESH,
        )

    gives = jnp.logical_and(h == 0, s >= 2)
    takes = base + 2 < n_space

    to_mate().start()

    @pl.when(gives)
    def _():
        vol_halo(0).start()
        vol_halo(1).start()

    for item in (0, 3, 1):
        send(item)

    owned = [
        pltpu.make_async_copy(src, dst, own.at[i])
        for i, (src, dst) in enumerate((
            (vol, volx.at[pl.ds(2 * h, 2)]),
            (w1.at[:, :, lanes], gat.at[me]),
            (m1, m1all.at[me]),
            (w2, w2all.at[me]),
            (m2, m2all.at[me]),
        ))
    ]
    for copy in owned:
        copy.start()
    owned[0].wait()
    to_mate().wait_recv()

    @pl.when(takes)
    def _():
        vol_halo(0).wait_recv()

    @pl.when(jnp.logical_not(takes))
    def _():
        volx[pl.ds(4, 1)] = jnp.zeros((1,) + volx.shape[1:], BF)

    pad[:, :, 8:9] = jnp.zeros((2, 5, 1) + pad.shape[3:], F32)
    x = volx[...].astype(F32)
    pad[0, :, 0:8] = x
    pad[1, :, 0:8] = jnp.concatenate([x[:, :, 1:], jnp.zeros_like(x[:, :, :1])], 2)
    for sd in range(2):
        for sr in range(2):
            for sc in range(2):
                v = pad[sc, sd : sd + 4, sr : sr + 8]
                xs[sd * 4 + sr * 2 + sc] = v.reshape(256, v.shape[-1]).astype(BF)

    def to_act(p):
        return pltpu.make_async_remote_copy(
            act_all.at[p, 1 - h], act_in.at[p], asem.at[p], arsem.at[p],
            device_id={"space": mate}, device_id_type=MESH,
        )

    def conv_pair(pd, pr):
        weight = lambda t: gat[:, t].reshape(-1, 128)
        for pc, acc in enumerate(pair_sum(xs, weight, pd, pr)):
            p = pd * 4 + pr * 2 + pc
            act_all[p] = silu(acc).astype(BF).reshape(2, 128, 128)
            to_act(p).start()

    def mix_phase(p):
        pd, pr, pc = p // 4, p // 2 % 2, p % 2
        to_act(p).wait_recv()
        r = jnp.dot(act_all[p, h], m1s[h], preferred_element_type=F32)
        r = r + jnp.dot(act_in[p], m1s[1 - h], preferred_element_type=F32)
        for d in range(2):
            for i in range(8):
                row = d * 64 + i * 8
                for half in range(2):
                    upf[2 * d + pd, 2 * i + pr, half, pl.ds(pc, 8, stride=2), :] = r[
                        row : row + 8, half * 128 : half * 128 + 128
                    ]

    forward(0)
    send(2)
    across(0)
    for copy in owned[1:]:
        copy.wait()
    forward(1)
    settle(0)
    conv_pair(0, 0)
    conv_pair(0, 1)
    forward(2)
    send(4)
    send(5)
    forward(3)
    across(1)
    across(2)
    settle(3)
    m1s[...] = m1all[...].reshape(2, 128, 256)
    for p in range(4):
        mix_phase(p)

    def emit(plane):
        for half in range(2):
            up[plane, 0:16, :, half * 128 : half * 128 + 128] = upf[plane, :, half].astype(BF)

    emit(0)

    def up_halo():
        return pltpu.make_async_remote_copy(
            up.at[0, pl.ds(0, 16)], halo, us.at[0], ur.at[0],
            device_id={"space": s - 1}, device_id_type=MESH,
        )

    @pl.when(s > 0)
    def _():
        up_halo().start()

    settle(1)
    settle(2)
    conv_pair(1, 0)
    conv_pair(1, 1)
    forward(4)
    forward(5)
    for p in range(4, 8):
        mix_phase(p)
    for plane in range(1, 4):
        emit(plane)
    up[:, 16:17] = jnp.zeros((5, 1) + up.shape[2:], BF)

    last = s + 1 == n_space

    @pl.when(last)
    def _():
        up[4, 0:16] = jnp.zeros(halo.shape, BF)

    @pl.when(jnp.logical_not(last))
    def _():
        up_halo().wait_recv()
        up[4, 0:16] = halo[...]

    across(4)
    settle(4)
    settle(5)

    def to_decoded(d):
        return pltpu.make_async_copy(
            planes.at[d], decoded.at[pl.ds(4 * d, 4)], outsem.at[d]
        )

    @pl.loop(0, 2)
    def _(d):
        second_block(d, up, w2all, m2all, planes.at[d], wide, views)
        to_decoded(d).start()

    for item in range(6):
        for k in range(n):
            core_copy(item, k).wait_send()
        if crosses(item):
            for k in (1, 2):
                straight(item, k).wait_send()
                around(item, k).wait_send()
        else:
            for k in range(1, n):
                to_peer(item, k).wait_send()
    to_mate().wait_send()
    for p in range(8):
        to_act(p).wait_send()

    @pl.when(gives)
    def _():
        vol_halo(0).wait_send()
        vol_halo(1).wait_send()

    @pl.when(s > 0)
    def _():
        up_halo().wait_send()

    for d in range(2):
        to_decoded(d).wait()


def second_block(d, up, w2, m2, out, wide, xs):
    for sd in range(2):
        x = up[pl.ds(2 * d + sd, 2)]
        moved = x.astype(F32)
        moved = jnp.concatenate([moved[:, :, 1:], jnp.zeros_like(moved[:, :, :1])], 2).astype(BF)
        for sr in range(2):
            xs[sd * 4 + sr * 2] = x[:, sr : sr + 16].reshape(512, 256)
            xs[sd * 4 + sr * 2 + 1] = moved[:, sr : sr + 16].reshape(512, 256)
    m = m2[...].reshape(128, 128)
    none = jnp.zeros_like(m)
    mixing = jnp.concatenate(
        [jnp.concatenate([m, none], 1), jnp.concatenate([none, m], 1)], 0
    )
    for pd in range(2):
        for pr in range(2):
            acc = jnp.concatenate(
                pair_sum(xs, lambda t: w2[:, t].reshape(256, 128), pd, pr), 1
            )
            r = jnp.dot(silu(acc).astype(BF), mixing, preferred_element_type=F32)
            for pc in range(2):
                for i in range(32):
                    wide[i // 16 * 2 + pd, i % 16 * 2 + pr, pl.ds(pc, 16, stride=2), :] = r[
                        i * 16 : i * 16 + 16, pc * 128 : pc * 128 + 128
                    ]
    out[...] = wide[...].astype(BF)


def per_device(n_dp, n_space, volume, conv_one, mix_one, conv_two, mix_two):
    n = n_dp // 2
    w1 = conv_one.reshape((27,) + conv_one.shape[3:])
    w2 = conv_two.reshape((27,) + conv_two.shape[3:])
    hbm = pl.BlockSpec(memory_space=pltpu.HBM)
    dma = pltpu.SemaphoreType.DMA
    decoded = pl.pallas_call(
        functools.partial(fused_kernel, n_dp, n_space),
        out_shape=jax.ShapeDtypeStruct((8, 32, 32, 128), BF),
        in_specs=[hbm] * 5,
        out_specs=hbm,
        scratch_shapes=[
            pltpu.VMEM((5, 17, 16, 256), BF),
            pltpu.VMEM((n_dp,) + w2.shape, BF),
            pltpu.VMEM((n_dp,) + mix_two.shape, BF),
            pltpu.VMEM((4, 32, 32, 128), F32),
            pltpu.VMEM((8, 512, 256), BF),
            pltpu.VMEM((2, 4, 32, 32, 128), BF),
            pltpu.VMEM((n_dp, 27, w1.shape[1], 128), BF),
            pltpu.VMEM((n_dp,) + mix_one.shape, BF),
            pltpu.VMEM((2, 128, 256), BF),
            pltpu.VMEM((5, 8, 8, 512), BF),
            pltpu.VMEM((2, 5, 9, 8, 512), F32),
            pltpu.VMEM((8, 256, 512), BF),
            pltpu.VMEM((8, 2, 128, 128), BF),
            pltpu.VMEM((8, 128, 128), BF),
            pltpu.VMEM((4, 16, 2, 16, 128), F32),
            pltpu.VMEM((16, 16, 256), BF),
            dma((6, n)), dma((6, n)), dma((6, n)), dma((6, n)),
            dma((1,)), dma((1,)), dma((2,)), dma((1,)),
            dma((8,)), dma((8,)), dma((1,)), dma((1,)), dma((5,)), dma((2,)),
        ],
        compiler_params=pltpu.CompilerParams(
            collective_id=0, has_side_effects=True, vmem_limit_bytes=60 * 2**20
        ),
    )(volume[0], w1, mix_one, w2, mix_two)
    return decoded[None]


def solution(mesh):
    return jax.shard_map(
        functools.partial(per_device, mesh.shape["dp"], mesh.shape["space"]),
        mesh=mesh,
        in_specs=(
            P("dp", "space", None, None, None),
            P(None, None, None, "dp", None),
            P("dp", None),
            P(None, None, None, "dp", None),
            P("dp", None),
        ),
        out_specs=P("dp", "space", None, None, None),
        check_vma=False,
    )
```

```python
import functools

import jax
import jax.numpy as jnp
from jax import lax
from jax.experimental import pallas as pl
from jax.experimental.pallas import tpu as pltpu
from jax.sharding import PartitionSpec as P

MESH = pl.DeviceIdType.MESH
BF = jnp.bfloat16
F32 = jnp.float32
PHASE_TAPS = (((1, 0),), ((2, 0), (0, 1)))
DEPTH_TAPS = (1, 2, 0)


def silu(v):
    u = 0.5 * v
    return u + u * jnp.tanh(u)


def pair_sum(xs, weight, pd, pr):
    both, extra = None, None
    for kd, sd in PHASE_TAPS[pd]:
        for kr, sr in PHASE_TAPS[pr]:
            t, sh = kd * 9 + kr * 3, sd * 4 + sr * 2
            wide = jnp.concatenate([weight(t + 1), weight(t + 2)], 1)
            a = jnp.dot(xs[sh], wide, preferred_element_type=F32)
            b = jnp.dot(xs[sh + 1], weight(t), preferred_element_type=F32)
            both = a if both is None else both + a
            extra = b if extra is None else extra + b
    return both[:, :128], both[:, 128:] + extra


def fused_kernel(
    n_dp, n_space, vol, w1, m1, w2, m2,
    decoded,
    up, w2all, m2all, wide, views, planes, gat, m1all, m1s, volx, pad, xs, act_all, act_in, upf, halo,
    ssem, rsem, fssem, frsem, vs, vr, hs, hr, asem, arsem, us, ur, own, outsem,
):
    n = n_dp // 2
    me = lax.axis_index("dp")
    s = lax.axis_index("space")
    q, core = me // 2, lax.rem(me, 2)
    sib = q * 2 + (1 - core)
    h = lax.rem(s, 2)
    mate = s + 1 - 2 * h
    base = s - h

    def peer(k):
        return lax.rem(q + k, n) * 2 + core

    def source(k):
        return lax.rem(q + n - k, n) * 2 + core

    def sib_source(k):
        return lax.rem(q + n - k, n) * 2 + (1 - core)

    barrier = pltpu.get_barrier_semaphore()
    for k in range(1, n):
        pl.semaphore_signal(barrier, inc=1, device_id={"dp": peer(k)}, device_id_type=MESH)
    pl.semaphore_signal(barrier, inc=1, device_id={"dp": sib}, device_id_type=MESH)
    greeted = n
    for k in (-2, -1, 1, 2):
        there = jnp.logical_and(s + k >= 0, s + k < n_space)
        greeted = greeted + there.astype(jnp.int32)

        @pl.when(there)
        def _(k=k):
            pl.semaphore_signal(
                barrier, inc=1, device_id={"space": s + k}, device_id_type=MESH
            )

    pl.semaphore_wait(barrier, greeted)

    lanes = pl.ds(pl.multiple_of(h * 128, 128), 128)

    def ends(item, slot):
        if item < 3:
            rows = pl.ds(DEPTH_TAPS[item] * 9, 9)
            return w1.at[rows, :, lanes], gat.at[slot, rows]
        mine, every = ((m1, m1all), (w2, w2all), (m2, m2all))[item - 3]
        return mine, every.at[slot]

    def to_peer(item, k):
        src, dst = ends(item, me)
        return pltpu.make_async_remote_copy(
            src, dst, ssem.at[item, k], rsem.at[item, k],
            device_id={"dp": peer(k)}, device_id_type=MESH,
        )

    def to_sib(item, k):
        if k == 0:
            src, dst = ends(item, me)
        else:
            _, dst = ends(item, source(k))
            src = dst
        return pltpu.make_async_remote_copy(
            src, dst, fssem.at[item, k], frsem.at[item, k],
            device_id={"dp": sib}, device_id_type=MESH,
        )

    flip = {
        1: q + 1 - 2 * lax.rem(q, 2),
        2: q + 2 - 4 * lax.rem(q // 2, 2),
    }

    def crosses(item):
        return n == 4 and item in (0, 1, 2, 4)

    def straight(item, k):
        src, dst = ends(item, me)
        return pltpu.make_async_remote_copy(
            src, dst, ssem.at[item, k], rsem.at[item, k],
            device_id={"dp": flip[k] * 2 + core}, device_id_type=MESH,
        )

    def half_of(item, chip, j):
        slot = chip * 2 + core
        if item < 3:
            rows = gat.shape[2] // 2
            return gat.at[slot, pl.ds(DEPTH_TAPS[item] * 9, 9), pl.ds(j * rows, rows)]
        return w2all.at[slot, pl.ds(14 * j, 14 - j)]

    def around(item, k):
        ref = half_of(item, flip[k], k - 1)
        sem = 3 * (k - 1)
        return pltpu.make_async_remote_copy(
            ref, ref, ssem.at[item, sem], rsem.at[item, sem],
            device_id={"dp": flip[3 - k] * 2 + core}, device_id_type=MESH,
        )

    def sib_from(item, k):
        chip = q if k == 0 else 3 - q if k == 3 else flip[k]
        src, dst = ends(item, chip * 2 + core)
        return pltpu.make_async_remote_copy(
            src if k == 0 else dst, dst, fssem.at[item, k], frsem.at[item, k],
            device_id={"dp": sib}, device_id_type=MESH,
        )

    def core_copy(item, k):
        return sib_from(item, k) if crosses(item) else to_sib(item, k)

    def send(item):
        if crosses(item):
            for k in (1, 2):
                straight(item, k).start()
        else:
            for k in range(1, n):
                to_peer(item, k).start()
        core_copy(item, 0).start()

    def forward(item):
        if crosses(item):
            for k in (1, 2):
                straight(item, k).wait_recv()
                around(item, k).start()
                core_copy(item, k).start()
        else:
            for k in range(1, n):
                to_peer(item, k).wait_recv()
                core_copy(item, k).start()

    def across(item):
        if crosses(item):
            for k in (1, 2):
                around(item, k).wait_recv()
            core_copy(item, 3).start()

    def settle(item):
        for k in range(n):
            core_copy(item, k).wait_recv()

    def to_mate():
        return pltpu.make_async_remote_copy(
            vol, volx.at[pl.ds(2 * h, 2)], vs.at[0], vr.at[0],
            device_id={"space": mate}, device_id_type=MESH,
        )

    def vol_halo(j):
        return pltpu.make_async_remote_copy(
            vol.at[pl.ds(0, 1)], volx.at[pl.ds(4, 1)], hs.at[j], hr.at[0],
            device_id={"space": s - 1 - j}, device_id_type=MESH,
        )

    gives = jnp.logical_and(h == 0, s >= 2)
    takes = base + 2 < n_space

    to_mate().start()

    @pl.when(gives)
    def _():
        vol_halo(0).start()
        vol_halo(1).start()

    for item in (0, 3, 1):
        send(item)

    owned = [
        pltpu.make_async_copy(src, dst, own.at[i])
        for i, (src, dst) in enumerate((
            (vol, volx.at[pl.ds(2 * h, 2)]),
            (w1.at[:, :, lanes], gat.at[me]),
            (m1, m1all.at[me]),
            (w2, w2all.at[me]),
            (m2, m2all.at[me]),
        ))
    ]
    for copy in owned:
        copy.start()
    owned[0].wait()
    to_mate().wait_recv()

    @pl.when(takes)
    def _():
        vol_halo(0).wait_recv()

    @pl.when(jnp.logical_not(takes))
    def _():
        volx[pl.ds(4, 1)] = jnp.zeros((1,) + volx.shape[1:], BF)

    pad[:, :, 8:9] = jnp.zeros((2, 5, 1) + pad.shape[3:], F32)
    x = volx[...].astype(F32)
    pad[0, :, 0:8] = x
    pad[1, :, 0:8] = jnp.concatenate([x[:, :, 1:], jnp.zeros_like(x[:, :, :1])], 2)
    for sd in range(2):
        for sr in range(2):
            for sc in range(2):
                v = pad[sc, sd : sd + 4, sr : sr + 8]
                xs[sd * 4 + sr * 2 + sc] = v.reshape(256, v.shape[-1]).astype(BF)

    def to_act(p):
        return pltpu.make_async_remote_copy(
            act_all.at[p, 1 - h], act_in.at[p], asem.at[p], arsem.at[p],
            device_id={"space": mate}, device_id_type=MESH,
        )

    def conv_pair(pd, pr):
        weight = lambda t: gat[:, t].reshape(-1, 128)
        for pc, acc in enumerate(pair_sum(xs, weight, pd, pr)):
            p = pd * 4 + pr * 2 + pc
            act_all[p] = silu(acc).astype(BF).reshape(2, 128, 128)
            to_act(p).start()

    def mix_phase(p):
        pd, pr, pc = p // 4, p // 2 % 2, p % 2
        to_act(p).wait_recv()
        r = jnp.dot(act_all[p, h], m1s[h], preferred_element_type=F32)
        r = r + jnp.dot(act_in[p], m1s[1 - h], preferred_element_type=F32)
        for d in range(2):
            for i in range(8):
                row = d * 64 + i * 8
                for half in range(2):
                    upf[2 * d + pd, 2 * i + pr, half, pl.ds(pc, 8, stride=2), :] = r[
                        row : row + 8, half * 128 : half * 128 + 128
                    ]

    forward(0)
    send(2)
    across(0)
    for copy in owned[1:]:
        copy.wait()
    forward(1)
    settle(0)
    conv_pair(0, 0)
    conv_pair(0, 1)
    forward(2)
    send(4)
    send(5)
    forward(3)
    across(1)
    across(2)
    settle(3)
    m1s[...] = m1all[...].reshape(2, 128, 256)
    for p in range(4):
        mix_phase(p)

    def emit(plane):
        for half in range(2):
            up[plane, 0:16, :, half * 128 : half * 128 + 128] = upf[plane, :, half].astype(BF)

    emit(0)

    def up_halo():
        return pltpu.make_async_remote_copy(
            up.at[0, pl.ds(0, 16)], halo, us.at[0], ur.at[0],
            device_id={"space": s - 1}, device_id_type=MESH,
        )

    @pl.when(s > 0)
    def _():
        up_halo().start()

    settle(1)
    settle(2)
    conv_pair(1, 0)
    conv_pair(1, 1)
    forward(4)
    forward(5)
    for p in range(4, 8):
        mix_phase(p)
    for plane in range(1, 4):
        emit(plane)
    up[:, 16:17] = jnp.zeros((5, 1) + up.shape[2:], BF)

    last = s + 1 == n_space

    @pl.when(last)
    def _():
        up[4, 0:16] = jnp.zeros(halo.shape, BF)

    @pl.when(jnp.logical_not(last))
    def _():
        up_halo().wait_recv()
        up[4, 0:16] = halo[...]

    across(4)
    settle(4)
    settle(5)

    def to_decoded(d):
        return pltpu.make_async_copy(
            planes.at[d], decoded.at[pl.ds(4 * d, 4)], outsem.at[d]
        )

    @pl.loop(0, 2)
    def _(d):
        second_block(d, up, w2all, m2all, planes.at[d], wide, views)
        to_decoded(d).start()

    for item in range(6):
        for k in range(n):
            core_copy(item, k).wait_send()
        if crosses(item):
            for k in (1, 2):
                straight(item, k).wait_send()
                around(item, k).wait_send()
        else:
            for k in range(1, n):
                to_peer(item, k).wait_send()
    to_mate().wait_send()
    for p in range(8):
        to_act(p).wait_send()

    @pl.when(gives)
    def _():
        vol_halo(0).wait_send()
        vol_halo(1).wait_send()

    @pl.when(s > 0)
    def _():
        up_halo().wait_send()

    for d in range(2):
        to_decoded(d).wait()


def second_block(d, up, w2, m2, out, wide, xs):
    for sd in range(2):
        x = up[pl.ds(2 * d + sd, 2)]
        moved = x.astype(F32)
        moved = jnp.concatenate([moved[:, :, 1:], jnp.zeros_like(moved[:, :, :1])], 2).astype(BF)
        for sr in range(2):
            xs[sd * 4 + sr * 2] = x[:, sr : sr + 16].reshape(512, 256)
            xs[sd * 4 + sr * 2 + 1] = moved[:, sr : sr + 16].reshape(512, 256)
    m = m2[...].reshape(128, 128)
    none = jnp.zeros_like(m)
    mixing = jnp.concatenate(
        [jnp.concatenate([m, none], 1), jnp.concatenate([none, m], 1)], 0
    )
    for pd in range(2):
        for pr in range(2):
            acc = jnp.concatenate(
                pair_sum(xs, lambda t: w2[:, t].reshape(256, 128), pd, pr), 1
            )
            r = jnp.dot(silu(acc).astype(BF), mixing, preferred_element_type=F32)
            for pc in range(2):
                for i in range(32):
                    wide[i // 16 * 2 + pd, i % 16 * 2 + pr, pl.ds(pc, 16, stride=2), :] = r[
                        i * 16 : i * 16 + 16, pc * 128 : pc * 128 + 128
                    ]
    out[...] = wide[...].astype(BF)


def per_device(n_dp, n_space, volume, conv_one, mix_one, conv_two, mix_two):
    n = n_dp // 2
    w1 = conv_one.reshape((27,) + conv_one.shape[3:])
    w2 = conv_two.reshape((27,) + conv_two.shape[3:])
    hbm = pl.BlockSpec(memory_space=pltpu.HBM)
    dma = pltpu.SemaphoreType.DMA
    decoded = pl.pallas_call(
        functools.partial(fused_kernel, n_dp, n_space),
        out_shape=jax.ShapeDtypeStruct((8, 32, 32, 128), BF),
        in_specs=[hbm] * 5,
        out_specs=hbm,
        scratch_shapes=[
            pltpu.VMEM((5, 17, 16, 256), BF),
            pltpu.VMEM((n_dp,) + w2.shape, BF),
            pltpu.VMEM((n_dp,) + mix_two.shape, BF),
            pltpu.VMEM((4, 32, 32, 128), F32),
            pltpu.VMEM((8, 512, 256), BF),
            pltpu.VMEM((2, 4, 32, 32, 128), BF),
            pltpu.VMEM((n_dp, 27, w1.shape[1], 128), BF),
            pltpu.VMEM((n_dp,) + mix_one.shape, BF),
            pltpu.VMEM((2, 128, 256), BF),
            pltpu.VMEM((5, 8, 8, 512), BF),
            pltpu.VMEM((2, 5, 9, 8, 512), F32),
            pltpu.VMEM((8, 256, 512), BF),
            pltpu.VMEM((8, 2, 128, 128), BF),
            pltpu.VMEM((8, 128, 128), BF),
            pltpu.VMEM((4, 16, 2, 16, 128), F32),
            pltpu.VMEM((16, 16, 256), BF),
            dma((6, n)), dma((6, n)), dma((6, n)), dma((6, n)),
            dma((1,)), dma((1,)), dma((2,)), dma((1,)),
            dma((8,)), dma((8,)), dma((1,)), dma((1,)), dma((5,)), dma((2,)),
        ],
        compiler_params=pltpu.CompilerParams(
            collective_id=0, has_side_effects=True, vmem_limit_bytes=60 * 2**20
        ),
    )(volume[0], w1, mix_one, w2, mix_two)
    return decoded[None]


def solution(mesh):
    return jax.shard_map(
        functools.partial(per_device, mesh.shape["dp"], mesh.shape["space"]),
        mesh=mesh,
        in_specs=(
            P("dp", "space", None, None, None),
            P(None, None, None, "dp", None),
            P("dp", None),
            P(None, None, None, "dp", None),
            P("dp", None),
        ),
        out_specs=P("dp", "space", None, None, None),
        check_vma=False,
    )
```
